256 devices in a mesh: seq: 32 (over x, z), dp: 8 (over y, core).
Axes of the slice: x: 4, y: 4, z: 8, core: 2. Of those that a mesh axis runs over, the one named last changes fastest.
Arguments:
- signal: bfloat16 [8, 16384, 768], P('dp', 'seq'), may hold values from -6 to 6
- first_kernel: bfloat16 [3, 768, 768], replicated, may hold values from -0.125 to 0.125
- second_kernel: bfloat16 [3, 768, 768], replicated, may hold values from -0.125 to 0.125
- cotangent: bfloat16 [8, 16384, 768], P('dp', 'seq'), may hold values from -6 to 6
Outputs:
- output: bfloat16 [8, 16384, 768], P('dp', 'seq')
- grad_signal: bfloat16 [8, 16384, 768], P('dp', 'seq')
- first_kernel_gradient: float32 [3, 768, 768], P(None, 'seq')
- second_kernel_gradient: float32 [3, 768, 768], P(None, 'seq')
The draws below stay inside these ranges and needn't reach their ends.
All inputs are finite; a program needn't handle non-finite values.
Results may differ from the reference program's by a relative error of at most 0.01.
Values may be sent and summed in bfloat16 or wider, within the bound.
No kernel may reach another device: no remote copies, remote signals or barrier semaphores. Data moves between devices by JAX's collectives and lax.ppermute only.
A program may use at most 128 MiB of HBM per device.

```python
import math
import jax
import jax.numpy as jnp
from jax import lax

CHANNELS = 768
FIRST_DILATION = 64
SECOND_DILATION = 128
BATCH = 8
WINDOW_BINS = 16384
TOKENS = 131072


def block_levels(rng, extent, shards, low, top_value):
    def one(dim, shards_of):
        draws = jax.random.uniform(jax.random.fold_in(jax.random.fold_in(rng, 6), dim), (shards_of,), jnp.float32, low / len(shards), top_value / len(shards))
        return jnp.repeat(jnp.exp(draws), extent[dim] // shards_of).reshape((-1,) + (1,) * (len(extent) - dim - 1))

    loudness = one(*shards[0])
    for cut in shards[1:]:
        loudness = loudness * one(*cut)
    return loudness


def scatter_about(key, extent, width, reach, pieces=(), kind=jnp.bfloat16):
    loudness = block_levels(key, extent, pieces, -0.22, 0.18) if pieces else 1.0
    values = jax.random.normal(key, extent, jnp.float32) * width * loudness
    return jnp.minimum(jnp.maximum(values, -reach), reach).astype(kind)


def setup_inputs(seed: int = 0) -> dict:
    key_of = jax.random.split(jax.random.key(seed), 5)
    signal = scatter_about(key_of[0], (BATCH, WINDOW_BINS, CHANNELS), 1.0, 6.0, ((0, 8), (1, 32)))
    first_kernel = scatter_about(key_of[1], (3, CHANNELS, CHANNELS), (3 * CHANNELS) ** -0.5, 0.125)
    second_kernel = scatter_about(key_of[2], (3, CHANNELS, CHANNELS), (3 * CHANNELS) ** -0.5, 0.125)
    cotangent = scatter_about(key_of[3], (BATCH, WINDOW_BINS, CHANNELS), 1.0, 6.0, ((0, 8), (1, 32)))
    return {"signal": signal, "first_kernel": first_kernel, "second_kernel": second_kernel, "cotangent": cotangent}


def gelu_tanh(v):
    return jax.nn.gelu(v, approximate=True)

def convolve_forward(padded_input, kernel_weight, dilation_step, element_count):
    total_sum = jnp.zeros((element_count, kernel_weight.shape[2]), jnp.float32)
    for tap_index in range(3):
        total_sum = total_sum + jnp.dot(padded_input[tap_index * dilation_step:tap_index * dilation_step + element_count], kernel_weight[tap_index], preferred_element_type=jnp.float32)
    return total_sum

def convolve_backward(gradient_padded, kernel_weight, dilation_step, element_count):
    total_sum = jnp.zeros((element_count, kernel_weight.shape[1]), jnp.float32)
    for tap_index in range(3):
        total_sum = total_sum + jnp.dot(gradient_padded[(2 - tap_index) * dilation_step:(2 - tap_index) * dilation_step + element_count], kernel_weight[tap_index].T, preferred_element_type=jnp.float32)
    return total_sum

def kernel_gradient(activation_padded, gradient_value, dilation_step, element_count):
    return jnp.stack([jnp.dot(activation_padded[tap_index * dilation_step:tap_index * dilation_step + element_count].T, gradient_value, preferred_element_type=jnp.float32) for tap_index in range(3)])

def reference(signal, first_kernel, second_kernel, cotangent):
    scale_factor = 1.0 / math.sqrt(TOKENS)

    def window(pair):
        sig, upstream_gradient = pair
        signal_float = sig.astype(jnp.float32)
        first_activation = gelu_tanh(signal_float).astype(jnp.bfloat16)
        first_margin = jnp.pad(first_activation, ((FIRST_DILATION, FIRST_DILATION), (0, 0)))
        hidden_state = (signal_float + convolve_forward(first_margin, first_kernel, FIRST_DILATION, WINDOW_BINS)).astype(jnp.bfloat16)
        middle_float = hidden_state.astype(jnp.float32)
        second_activation = gelu_tanh(middle_float).astype(jnp.bfloat16)
        second_margin = jnp.pad(second_activation, ((SECOND_DILATION, SECOND_DILATION), (0, 0)))
        output = (middle_float + convolve_forward(second_margin, second_kernel, SECOND_DILATION, WINDOW_BINS)).astype(jnp.bfloat16)
        upstream_padded = jnp.pad(upstream_gradient, ((SECOND_DILATION, SECOND_DILATION), (0, 0)))
        second_backward = convolve_backward(upstream_padded, second_kernel, SECOND_DILATION, WINDOW_BINS)
        _, pull_b = jax.vjp(gelu_tanh, middle_float)
        middle_gradient = (upstream_gradient.astype(jnp.float32) + pull_b(second_backward)[0]).astype(jnp.bfloat16)
        second_portion = kernel_gradient(second_margin, upstream_gradient, SECOND_DILATION, WINDOW_BINS) * scale_factor
        middle_padded = jnp.pad(middle_gradient, ((FIRST_DILATION, FIRST_DILATION), (0, 0)))
        first_backward = convolve_backward(middle_padded, first_kernel, FIRST_DILATION, WINDOW_BINS)
        _, pull_a = jax.vjp(gelu_tanh, signal_float)
        grad_sig = (middle_gradient.astype(jnp.float32) + pull_a(first_backward)[0]).astype(jnp.bfloat16)
        first_portion = kernel_gradient(first_margin, middle_gradient, FIRST_DILATION, WINDOW_BINS) * scale_factor
        return (output, grad_sig, first_portion, second_portion)
    output, grad_signal, parts_a, parts_b = lax.map(window, (signal, cotangent))
    return (output, grad_signal, lax.optimization_barrier(jnp.sum(parts_a, axis=0)), lax.optimization_barrier(jnp.sum(parts_b, axis=0)))
```

```python
import math

import jax
import jax.numpy as jnp
from jax import lax
from jax.experimental import pallas as pl
from jax.experimental.pallas import tpu as pltpu
from jax.sharding import Mesh, PartitionSpec as P

FIRST = 64
SECOND = 128
CUBIC = 0.044715
ROOT = math.sqrt(2.0 / math.pi)
F32 = jnp.float32
BF16 = jnp.bfloat16


def gelu(v):
    return 0.5 * v * (1.0 + jnp.tanh(ROOT * (v + CUBIC * v * v * v)))


def gelu_both(v):
    square = v * v
    t = jnp.tanh(ROOT * v * (1.0 + CUBIC * square))
    half = 0.5 * (1.0 + t)
    slope = half + 0.5 * v * (1.0 - t * t) * (ROOT * (1.0 + 3.0 * CUBIC * square))
    return v * half, slope


def dot(a, b):
    return jnp.dot(a, b, preferred_element_type=F32)


def dot_nt(a, b):
    return lax.dot_general(a, b, (((1,), (1,)), ((), ())), preferred_element_type=F32)


def dot_tn(a, b):
    return lax.dot_general(a, b, (((0,), (0,)), ((), ())), preferred_element_type=F32)


def front_kernel(act, cot_ext, sig, cot, w1, w2, middle, act_b, grad_m, fwd, back):
    rows = sig.shape[0]
    total = dot(act[0:rows], w1[0])
    for k in (1, 2):
        total = total + dot(act[k * FIRST : k * FIRST + rows], w1[k])
    fwd[...] = total
    total = dot_nt(cot_ext[2 * SECOND : 2 * SECOND + rows], w2[0])
    for k in (1, 2):
        start = (2 - k) * SECOND
        total = total + dot_nt(cot_ext[start : start + rows], w2[k])
    back[...] = total

    @pl.loop(0, rows // 64)
    def _(i):
        at = pl.ds(pl.multiple_of(i * 64, 64), 64)
        mid = (sig[at].astype(F32) + fwd[at]).astype(BF16)
        middle[at] = mid
        value, slope = gelu_both(mid.astype(F32))
        act_b[at] = value.astype(BF16)
        grad_m[at] = (cot[at].astype(F32) + slope * back[at]).astype(BF16)


def front(act_ext, cot_ext, sig, cot, w1, w2):
    rows, ch = sig.shape
    tile = 256
    full = lambda a: pl.BlockSpec(a.shape, lambda n: (0, 0))
    cols = pl.BlockSpec((rows, tile), lambda n: (0, n))
    out = jax.ShapeDtypeStruct((rows, ch), BF16)
    return pl.pallas_call(
        front_kernel,
        grid=(ch // tile,),
        in_specs=[
            full(act_ext),
            full(cot_ext),
            cols,
            cols,
            pl.BlockSpec((3, ch, tile), lambda n: (0, 0, n)),
            pl.BlockSpec((3, tile, ch), lambda n: (0, n, 0)),
        ],
        out_specs=[cols, cols, cols],
        out_shape=[out, out, out],
        scratch_shapes=[pltpu.VMEM((rows, tile), F32), pltpu.VMEM((rows, tile), F32)],
        compiler_params=pltpu.CompilerParams(vmem_limit_bytes=40 << 20),
        cost_estimate=pl.CostEstimate(
            flops=12 * rows * ch * ch, transcendentals=rows * ch, bytes_accessed=14 * ch * ch
        ),
        name="front",
    )(act_ext, cot_ext, sig, cot, w1, w2)


def back_kernel(act_b, lo, hi, grad_m, mid, sig, gm, w1, w2, output, grad_s, a_ext, g_ext, fwd, bwd):
    rows = mid.shape[0]

    @pl.when(pl.program_id(0) == 0)
    def _():
        a_ext[0:SECOND] = lo[0:SECOND]
        a_ext[SECOND : SECOND + rows] = act_b[...]
        a_ext[SECOND + rows :] = hi[0:SECOND]
        g_ext[0:FIRST] = lo[SECOND:]
        g_ext[FIRST : FIRST + rows] = grad_m[...]
        g_ext[FIRST + rows :] = hi[SECOND:]

    total = dot(a_ext[0:rows], w2[0])
    for k in (1, 2):
        total = total + dot(a_ext[k * SECOND : k * SECOND + rows], w2[k])
    fwd[...] = total
    total = dot_nt(g_ext[2 * FIRST : 2 * FIRST + rows], w1[0])
    for k in (1, 2):
        start = (2 - k) * FIRST
        total = total + dot_nt(g_ext[start : start + rows], w1[k])
    bwd[...] = total

    @pl.loop(0, rows // 64)
    def _(i):
        at = pl.ds(pl.multiple_of(i * 64, 64), 64)
        output[at] = (mid[at].astype(F32) + fwd[at]).astype(BF16)
        _, slope = gelu_both(sig[at].astype(F32))
        grad_s[at] = (gm[at].astype(F32) + slope * bwd[at]).astype(BF16)


def back(act_b, lo, hi, grad_m, mid, sig, w1, w2):
    rows, ch = sig.shape
    tile = 256
    full = lambda a: pl.BlockSpec(a.shape, lambda n: (0, 0))
    cols = pl.BlockSpec((rows, tile), lambda n: (0, n))
    out = jax.ShapeDtypeStruct((rows, ch), BF16)
    return pl.pallas_call(
        back_kernel,
        grid=(ch // tile,),
        in_specs=[
            full(act_b),
            full(lo),
            full(hi),
            full(grad_m),
            cols,
            cols,
            cols,
            pl.BlockSpec((3, tile, ch), lambda n: (0, n, 0)),
            pl.BlockSpec((3, ch, tile), lambda n: (0, 0, n)),
        ],
        out_specs=[cols, cols],
        out_shape=[out, out],
        scratch_shapes=[
            pltpu.VMEM((rows + 2 * SECOND, ch), BF16),
            pltpu.VMEM((rows + 2 * FIRST, ch), BF16),
            pltpu.VMEM((rows, tile), F32),
            pltpu.VMEM((rows, tile), F32),
        ],
        compiler_params=pltpu.CompilerParams(vmem_limit_bytes=40 << 20),
        cost_estimate=pl.CostEstimate(
            flops=12 * rows * ch * ch, transcendentals=rows * ch, bytes_accessed=14 * ch * ch
        ),
        name="rear",
    )(act_b, lo, hi, grad_m, mid, sig, grad_m, w1, w2)


def weight_kernel(
    parts, core, act_b, act_ext, f_all, e_all, grad_t, cot_t, f_t, e_t, out
):
    nx, ny, nz, units = parts
    rows = act_b.shape[0]
    n = pl.program_id(0)

    def emit(left_own, left_far, right_own, right_far, left_at, right_at):
        for k in range(3):
            a, b = left_at(k), right_at(k)
            total = dot_tn(left_own[a : a + rows], right_own[b : b + rows])
            total = total + dot_tn(left_far[a : a + rows], right_far[b : b + rows])
            for j in range(2):
                tile = total[:, j * 128 : (j + 1) * 128].astype(BF16).reshape(nx, nz, 3, 8, 128)
                for g in range(3):
                    unit = k * 18 + (2 * n + j) * 3 + g
                    out[:, unit // units, :, unit % units] = tile[:, :, g]

    @pl.when(n == 0)
    def _():
        out[:, ny - 1, :, units - 2 :] = jnp.zeros((nx, nz, 2, 8, 128), BF16)

    @pl.when(core[0] == 0)
    def _():
        emit(act_b, f_all, cot_t, e_t, lambda k: 0, lambda k: (2 - k) * SECOND)

    @pl.when(core[0] != 0)
    def _():
        emit(act_ext, e_all, grad_t, f_t, lambda k: k * FIRST, lambda k: 0)


def weights(parts, core, act_b, act_ext, f_all, e_all, grad_m, cot_ext):
    rows, ch = act_b.shape
    tile = 256
    nx, ny, nz, units = parts
    full = lambda a: pl.BlockSpec(a.shape, lambda n: (0, 0))
    cols = lambda a: pl.BlockSpec((a.shape[0], tile), lambda n: (0, n))
    shape = (nx, ny, nz, units, 8, 128)
    return pl.pallas_call(
        lambda *refs: weight_kernel(parts, *refs),
        grid=(ch // tile,),
        in_specs=[
            pl.BlockSpec(memory_space=pltpu.SMEM),
            full(act_b),
            full(act_ext),
            full(f_all),
            full(e_all),
            cols(grad_m),
            cols(cot_ext),
            cols(f_all),
            cols(e_all),
        ],
        out_specs=pl.BlockSpec(shape, lambda n: (0,) * 6),
        out_shape=jax.ShapeDtypeStruct(shape, BF16),
        compiler_params=pltpu.CompilerParams(vmem_limit_bytes=48 << 20),
        cost_estimate=pl.CostEstimate(
            flops=12 * rows * ch * ch, transcendentals=0, bytes_accessed=12 * ch * ch
        ),
        name="weights",
    )(core, act_b, act_ext, f_all, e_all, grad_m, cot_ext, f_all, e_all)


def neighbours(low, high):
    axes = ("x", "z")
    count = lax.axis_size("x") * lax.axis_size("z")
    forward = [(i, i + 1) for i in range(count - 1)]
    backward = [(t, s) for s, t in forward]
    return lax.ppermute(high, axes, forward), lax.ppermute(low, axes, backward)


def per_device(signal, w1, w2, cotangent):
    sig, cot = signal[0], cotangent[0]
    rows, ch = sig.shape
    nx, ny, nz = (lax.axis_size(a) for a in ("x", "y", "z"))
    tokens = signal.shape[0] * ny * lax.axis_size("c") * rows * nx * nz
    scale = 1.0 / math.sqrt(tokens)
    groups = ch // (nx * nz) // 8
    count = 3 * (ch // 128) * groups
    units = -(-count // ny)
    core = lax.axis_index("c")

    lo, hi = neighbours(
        jnp.concatenate([sig[:FIRST], cot[:SECOND]]),
        jnp.concatenate([sig[rows - FIRST :], cot[rows - SECOND :]]),
    )
    act = lambda v: gelu(v.astype(F32)).astype(BF16)
    act_ext = jnp.concatenate([act(lo[:FIRST]), act(sig), act(hi[:FIRST])])
    cot_ext = jnp.concatenate([lo[FIRST:], cot, hi[FIRST:]])
    pad = cot_ext.shape[0] - act_ext.shape[0]
    swap = [(0, 1), (1, 0)]
    e_all = lax.ppermute(
        jnp.where(core == 0, jnp.pad(act_ext, ((0, pad), (0, 0))), cot_ext), "c", swap
    )
    mid, act_b, grad_m = front(act_ext, cot_ext, sig, cot, w1, w2)
    f_all = lax.ppermute(jnp.where(core == 0, grad_m, act_b), "c", swap)
    lo2, hi2 = neighbours(
        jnp.concatenate([act_b[:SECOND], grad_m[:FIRST]]),
        jnp.concatenate([act_b[rows - SECOND :], grad_m[rows - FIRST :]]),
    )
    parts = (nx, ny, nz, units)
    piece = weights(
        parts, core.astype(jnp.int32).reshape(1), act_b, act_ext, f_all, e_all, grad_m, cot_ext
    )
    output, grad_s = back(act_b, lo2, hi2, grad_m, mid, sig, w1, w2)

    got = lax.all_to_all(piece.reshape(nx * ny, nz, units, 8, 128), ("x", "y"), 0, 0, tiled=True)
    part = jnp.sum(got.astype(F32), axis=0).astype(BF16)
    got = lax.all_to_all(part, "z", 0, 0, tiled=True)
    part = jnp.sum(got.astype(F32), axis=0).astype(BF16)
    both = lax.all_to_all(
        jnp.broadcast_to(part[None], (2 * ny, units, 8, 128)), ("y", "c"), 0, 0, tiled=True
    )
    both = both.reshape(ny, 2, units, 8, 128)

    def assemble(layer):
        flat = both[:, layer].reshape(ny * units, 8, 128)[:count]
        flat = flat.reshape(3, ch // 128, groups, 8, 128).transpose(0, 2, 3, 1, 4)
        return flat.reshape(3, groups * 8, ch).astype(F32) * scale

    return output[None], grad_s[None], assemble(1), assemble(0)


def solution(mesh):
    fine = Mesh(mesh.devices.reshape(4, 8, 4, 2), ("x", "z", "y", "c"))
    placed = P(("y", "c"), ("x", "z"), None)
    split = P(None, ("x", "z"), None)
    return jax.shard_map(
        per_device,
        mesh=fine,
        in_specs=(placed, P(), P(), placed),
        out_specs=(placed, placed, split, split),
        check_vma=False,
    )
```

```python
import math

import jax
import jax.numpy as jnp
from jax import lax
from jax.experimental import pallas as pl
from jax.experimental.pallas import tpu as pltpu
from jax.sharding import Mesh, PartitionSpec as P

FIRST = 64
SECOND = 128
CUBIC = 0.044715
ROOT = math.sqrt(2.0 / math.pi)
F32 = jnp.float32
BF16 = jnp.bfloat16


def gelu(v):
    return 0.5 * v * (1.0 + jnp.tanh(ROOT * (v + CUBIC * v * v * v)))


def gelu_both(v):
    square = v * v
    t = jnp.tanh(ROOT * v * (1.0 + CUBIC * square))
    half = 0.5 * (1.0 + t)
    slope = half + 0.5 * v * (1.0 - t * t) * (ROOT * (1.0 + 3.0 * CUBIC * square))
    return v * half, slope


def dot(a, b):
    return jnp.dot(a, b, preferred_element_type=F32)


def dot_nt(a, b):
    return lax.dot_general(a, b, (((1,), (1,)), ((), ())), preferred_element_type=F32)


def dot_tn(a, b):
    return lax.dot_general(a, b, (((0,), (0,)), ((), ())), preferred_element_type=F32)


def in_hbm(a):
    return pltpu.with_memory_space_constraint(a, pltpu.HBM)


def in_vmem(a):
    return pltpu.with_memory_space_constraint(a, pltpu.VMEM)


def edges(sig, cot):
    rows = sig.shape[0]

    def body(sig, cot, low, high, low_far, high_far, sems):
        pairs = []
        for first, last, skip_s, skip_c, take_s in (
            (low, high, 0, 0, FIRST),
            (low_far, high_far, FIRST, SECOND, SECOND),
        ):
            take_c = FIRST + SECOND - take_s
            pairs += [
                (sig, skip_s, first, 0, take_s),
                (cot, skip_c, first, take_s, take_c),
                (sig, rows - skip_s - take_s, last, 0, take_s),
                (cot, rows - skip_c - take_c, last, take_s, take_c),
            ]
        copies = [
            pltpu.make_async_copy(src.at[pl.ds(a, n)], dst.at[pl.ds(b, n)], sems.at[i])
            for i, (src, a, dst, b, n) in enumerate(pairs)
        ]
        for copy in copies:
            copy.start()
        for copy in copies:
            copy.wait()

    out = pltpu.VMEM((FIRST + SECOND, sig.shape[1]), BF16)
    return pl.pallas_call(
        body,
        in_specs=[pl.BlockSpec(memory_space=pl.ANY)] * 2,
        out_specs=[pl.BlockSpec(memory_space=pltpu.VMEM)] * 4,
        out_shape=[out] * 4,
        scratch_shapes=[pltpu.SemaphoreType.DMA((8,))],
        compiler_params=pltpu.CompilerParams(vmem_limit_bytes=2 << 20),
        name="edges",
    )(in_hbm(sig), in_hbm(cot))


def once(a):
    return pl.BlockSpec(a.shape, lambda n: (0, 0), pipeline_mode=pl.Buffered(1))


def three_taps(dots, left, weight, starts, rows):
    total = dots(left[starts[0] : starts[0] + rows], weight[0])
    for k in (1, 2):
        total = total + dots(left[starts[k] : starts[k] + rows], weight[k])
    return total


def front_kernel(core, act, cot_ext, sig, cot, w1, w2, middle, act_b, grad_m, swap, fwd, bwd):
    rows = sig.shape[0]
    fwd[...] = three_taps(dot, act, w1, [k * FIRST for k in range(3)], rows)
    bwd[...] = three_taps(dot_nt, cot_ext, w2, [(2 - k) * SECOND for k in range(3)], rows)

    @pl.loop(0, rows // 64)
    def _(i):
        at = pl.ds(pl.multiple_of(i * 64, 64), 64)
        mid = (sig[at].astype(F32) + fwd[at]).astype(BF16)
        middle[at] = mid
        value, slope = gelu_both(mid.astype(F32))
        grad = cot[at].astype(F32) + slope * bwd[at]
        act_b[at] = value.astype(BF16)
        grad_m[at] = grad.astype(BF16)
        swap[at] = jnp.where(core[0] == 0, grad, value).astype(BF16)


def front(core, act_ext, cot_ext, sig, cot, w1, w2):
    rows, ch = sig.shape
    tile = 256
    cols = pl.BlockSpec((rows, tile), lambda n: (0, n))
    out = jax.ShapeDtypeStruct((rows, ch), BF16)
    return pl.pallas_call(
        front_kernel,
        grid=(ch // tile,),
        in_specs=[
            pl.BlockSpec(memory_space=pltpu.SMEM),
            once(act_ext),
            once(cot_ext),
            cols,
            cols,
            pl.BlockSpec((3, ch, tile), lambda n: (0, 0, n)),
            pl.BlockSpec((3, tile, ch), lambda n: (0, n, 0)),
        ],
        out_specs=[cols] * 4,
        out_shape=[out] * 4,
        scratch_shapes=[pltpu.VMEM((rows, tile), F32), pltpu.VMEM((rows, tile), F32)],
        compiler_params=pltpu.CompilerParams(vmem_limit_bytes=16 << 20),
        cost_estimate=pl.CostEstimate(
            flops=12 * rows * ch * ch, transcendentals=rows * ch, bytes_accessed=14 * ch * ch
        ),
        name="front",
    )(core, act_ext, cot_ext, sig, cot, in_hbm(w1), in_hbm(w2))


def wing_kernel(inside, act, cot_ext, lo, hi, lo_far, hi_far, sig_t, cot_t, w1, w2, low, high, a_ext, c_ext):
    rows = act.shape[0] - 2 * FIRST

    @pl.when(pl.program_id(0) == 0)
    def _():
        far_low = gelu(lo_far[0:SECOND].astype(F32)).astype(BF16)
        far_high = gelu(hi_far[0:SECOND].astype(F32)).astype(BF16)
        a_ext[0, 0:SECOND] = far_low
        a_ext[0, SECOND:] = act[rows : rows + SECOND]
        a_ext[1, 0:FIRST] = far_low[FIRST:]
        a_ext[1, FIRST:SECOND] = act[0:FIRST]
        a_ext[1, SECOND : SECOND + FIRST] = act[rows + FIRST : rows + SECOND]
        a_ext[1, SECOND + FIRST :] = far_high[0:FIRST]
        a_ext[2, 0:SECOND] = act[0:SECOND]
        a_ext[2, SECOND:] = far_high
        c_ext[2, 0:FIRST] = lo_far[SECOND:]
        c_ext[2, FIRST:] = cot_ext[rows : rows + FIRST]
        c_ext[1, 0:FIRST] = cot_ext[FIRST:SECOND]
        c_ext[1, FIRST:] = cot_ext[rows + SECOND : rows + SECOND + FIRST]
        c_ext[0, 0:FIRST] = cot_ext[SECOND + FIRST : 2 * SECOND]
        c_ext[0, FIRST:] = hi_far[SECOND:]

    total = dot(a_ext[0], w1[0])
    for k in (1, 2):
        total = total + dot(a_ext[k], w1[k])
    mid = (sig_t[...].astype(F32) + total).astype(BF16).astype(F32)
    value, slope = gelu_both(mid)
    total = dot_nt(c_ext[0], w2[0])
    for k in (1, 2):
        total = total + dot_nt(c_ext[k], w2[k])
    slope = slope[SECOND - FIRST : SECOND + FIRST]
    grad = cot_t[...].astype(F32) + slope * total
    low[0:SECOND] = jnp.where(inside[0] > 0, value[0:SECOND], 0.0).astype(BF16)
    low[SECOND:] = jnp.where(inside[0] > 0, grad[0:FIRST], 0.0).astype(BF16)
    high[0:SECOND] = jnp.where(inside[1] > 0, value[SECOND:], 0.0).astype(BF16)
    high[SECOND:] = jnp.where(inside[1] > 0, grad[FIRST:], 0.0).astype(BF16)


def wings(inside, act_ext, cot_ext, lo, hi, lo_far, hi_far, w1, w2):
    ch = act_ext.shape[1]
    tile = 256
    size = FIRST + SECOND
    sig_t = jnp.concatenate([lo_far[FIRST:SECOND], lo[:FIRST], hi[:FIRST], hi_far[: SECOND - FIRST]])
    cot_t = jnp.concatenate([lo[FIRST + SECOND - FIRST :], hi[FIRST : 2 * FIRST]])
    cols = lambda a: pl.BlockSpec((a.shape[0], tile), lambda n: (0, n))
    out = jax.ShapeDtypeStruct((size, ch), BF16)
    return pl.pallas_call(
        wing_kernel,
        grid=(ch // tile,),
        in_specs=[
            pl.BlockSpec(memory_space=pltpu.SMEM),
            *[once(a) for a in (act_ext, cot_ext, lo, hi, lo_far, hi_far)],
            cols(sig_t),
            cols(cot_t),
            pl.BlockSpec((3, ch, tile), lambda n: (0, 0, n)),
            pl.BlockSpec((3, tile, ch), lambda n: (0, n, 0)),
        ],
        out_specs=[cols(out), cols(out)],
        out_shape=[out, out],
        scratch_shapes=[
            pltpu.VMEM((3, 2 * SECOND, ch), BF16),
            pltpu.VMEM((3, 2 * FIRST, ch), BF16),
        ],
        compiler_params=pltpu.CompilerParams(vmem_limit_bytes=16 << 20),
        cost_estimate=pl.CostEstimate(
            flops=6 * (2 * SECOND + 2 * FIRST) * ch * ch,
            transcendentals=4 * SECOND * ch,
            bytes_accessed=12 * ch * ch,
        ),
        name="wings",
    )(inside, act_ext, cot_ext, lo, hi, lo_far, hi_far, sig_t, cot_t, w1, w2)


def back_kernel(act_b, lo, hi, grad_m, mid, sig, gm, w1, w2, output, grad_s, a_ext, g_ext, fwd, bwd):
    rows = mid.shape[0]

    @pl.when(pl.program_id(0) == 0)
    def _():
        a_ext[0:SECOND] = lo[0:SECOND]
        a_ext[SECOND : SECOND + rows] = act_b[...]
        a_ext[SECOND + rows :] = hi[0:SECOND]
        g_ext[0:FIRST] = lo[SECOND:]
        g_ext[FIRST : FIRST + rows] = grad_m[...]
        g_ext[FIRST + rows :] = hi[SECOND:]

    total = dot(a_ext[0:rows], w2[0])
    for k in (1, 2):
        total = total + dot(a_ext[k * SECOND : k * SECOND + rows], w2[k])
    fwd[...] = total
    total = dot_nt(g_ext[2 * FIRST : 2 * FIRST + rows], w1[0])
    for k in (1, 2):
        start = (2 - k) * FIRST
        total = total + dot_nt(g_ext[start : start + rows], w1[k])
    bwd[...] = total

    @pl.loop(0, rows // 64)
    def _(i):
        at = pl.ds(pl.multiple_of(i * 64, 64), 64)
        output[at] = (mid[at].astype(F32) + fwd[at]).astype(BF16)
        _, slope = gelu_both(sig[at].astype(F32))
        grad_s[at] = (gm[at].astype(F32) + slope * bwd[at]).astype(BF16)


def back(act_b, lo, hi, grad_m, mid, sig, w1, w2):
    rows, ch = sig.shape
    tile = 256
    cols = pl.BlockSpec((rows, tile), lambda n: (0, n))
    out = jax.ShapeDtypeStruct((rows, ch), BF16)
    return pl.pallas_call(
        back_kernel,
        grid=(ch // tile,),
        in_specs=[
            once(act_b),
            once(lo),
            once(hi),
            once(grad_m),
            cols,
            cols,
            cols,
            pl.BlockSpec((3, tile, ch), lambda n: (0, n, 0)),
            pl.BlockSpec((3, ch, tile), lambda n: (0, 0, n)),
        ],
        out_specs=[cols, cols],
        out_shape=[out, out],
        scratch_shapes=[
            pltpu.VMEM((rows + 2 * SECOND, ch), BF16),
            pltpu.VMEM((rows + 2 * FIRST, ch), BF16),
            pltpu.VMEM((rows, tile), F32),
            pltpu.VMEM((rows, tile), F32),
        ],
        compiler_params=pltpu.CompilerParams(vmem_limit_bytes=16 << 20),
        cost_estimate=pl.CostEstimate(
            flops=12 * rows * ch * ch, transcendentals=rows * ch, bytes_accessed=14 * ch * ch
        ),
        name="rear",
    )(act_b, lo, hi, grad_m, mid, sig, grad_m, w1, w2)


def weight_kernel(parts, lead_x, core, act_b, act_ext, f_all, far_act, right_l2, far_l2, right_l1, far_l1, out):
    nx, ny, nz, units = parts
    rows = act_b.shape[0]

    def emit(left_own, left_far, right_own, right_far, left_at, right_at):
        for k in range(3):
            a, b = left_at(k), right_at(k)
            total = dot_tn(left_own[a : a + rows], right_own[b : b + rows])
            total = total + dot_tn(left_far[a : a + rows], right_far[b : b + rows])
            for j in range(3):
                tile = total[:, j * 128 : (j + 1) * 128].astype(BF16).reshape(nx, nz, 3, 8, 128)
                for g in range(3):
                    unit = k * 9 + j * 3 + g
                    y, i = unit // units, unit % units
                    if lead_x:
                        out[:, y, :, i] = tile[:, :, g]
                    else:
                        out[y, :, :, i] = tile[:, :, g]

    blank = jnp.zeros((nx, nz, 8, 128), BF16)
    if lead_x:
        out[:, ny - 1, :, units - 1] = blank
    else:
        out[ny - 1, :, :, units - 1] = blank

    @pl.when(core[0] == 0)
    def _():
        emit(act_b, f_all, right_l2, far_l2, lambda k: 0, lambda k: (2 - k) * SECOND)

    @pl.when(core[0] != 0)
    def _():
        emit(act_ext, far_act, right_l1, far_l1, lambda k: k * FIRST, lambda k: 0)


def weights(parts, half, core, act_b, act_ext, f_all, far_act, far_cot, grad_m, cot_ext):
    rows, ch = act_b.shape
    tile = ch // 2
    nx, ny, nz, units = parts
    cols = lambda a: pl.BlockSpec(
        (a.shape[0], tile), lambda n: (0, half), pipeline_mode=pl.Buffered(1)
    )
    shape = ((nx, ny) if half == 0 else (ny, nx)) + (nz, units, 8, 128)
    return pl.pallas_call(
        lambda *refs: weight_kernel(parts, half == 0, *refs),
        grid=(1,),
        in_specs=[
            pl.BlockSpec(memory_space=pltpu.SMEM),
            once(act_b),
            once(act_ext),
            once(f_all),
            once(far_act),
            cols(cot_ext),
            cols(far_cot),
            cols(grad_m),
            cols(f_all),
        ],
        out_specs=pl.BlockSpec(shape, lambda n: (0,) * 6),
        out_shape=pltpu.VMEM(shape, BF16),
        compiler_params=pltpu.CompilerParams(vmem_limit_bytes=16 << 20),
        cost_estimate=pl.CostEstimate(
            flops=6 * rows * ch * ch, transcendentals=0, bytes_accessed=6 * ch * ch
        ),
        name="weights",
    )(core, act_b, act_ext, f_all, far_act, cot_ext, far_cot, grad_m, f_all)


def exchange(data, axis, order):
    n = lax.axis_size(axis)
    rest = data.shape[1:]
    total = None
    for k in (0, 1, n - 1, *range(2, n - 1)):
        chunk = lax.dynamic_slice(
            data, (order[k],) + (0,) * len(rest), (1,) + rest, allow_negative_indices=False
        ).reshape(rest)
        if k:
            chunk = lax.ppermute(chunk, axis, [(i, (i + k) % n) for i in range(n)])
        chunk = chunk.astype(F32)
        total = chunk if total is None else total + chunk
    return total.astype(BF16)


def order_of(axis):
    n = lax.axis_size(axis)
    me = lax.axis_index(axis).astype(jnp.int32)
    return [jnp.where(me + k < n, me + k, me + k - n) for k in range(n)]


def neighbours(low, high):
    axes = ("x", "z")
    count = lax.axis_size("x") * lax.axis_size("z")
    forward = [(i, i + 1) for i in range(count - 1)]
    backward = [(t, s) for s, t in forward]
    return lax.ppermute(high, axes, forward), lax.ppermute(low, axes, backward)


def per_device(signal, w1, w2, cotangent):
    sig, cot = signal[0], cotangent[0]
    rows, ch = sig.shape
    nx, ny, nz = (lax.axis_size(a) for a in ("x", "y", "z"))
    tokens = signal.shape[0] * ny * lax.axis_size("c") * rows * nx * nz
    scale = 1.0 / math.sqrt(tokens)
    units = -(-27 // ny)
    core = lax.axis_index("c").astype(jnp.int32).reshape(1)
    place = lax.axis_index("x") * nz + lax.axis_index("z")
    inside = jnp.stack([place > 0, place < nx * nz - 1]).astype(jnp.int32)

    order_x, order_y = order_of("x"), order_of("y")
    sig, cot, core, inside, order_x, order_y = lax.optimization_barrier(
        (sig, cot, core, inside, order_x, order_y)
    )

    low, high, low_far, high_far = edges(sig, cot)
    lo, hi = neighbours(low, high)
    lo_far, hi_far = neighbours(low_far, high_far)
    act = lambda v: gelu(v.astype(F32)).astype(BF16)
    act_ext = jnp.concatenate([act(lo[:FIRST]), act(sig), act(hi[:FIRST])])
    cot_ext = jnp.concatenate([lo[FIRST:], cot, hi[FIRST:]])
    swap = lambda a: lax.ppermute(a, "c", [(0, 1), (1, 0)])
    far_act, far_cot = swap(act_ext), swap(cot_ext)
    mid, act_b, grad_m, give = front(core, act_ext, cot_ext, sig, cot, w1, w2)
    f_all = swap(give)
    parts = (nx, ny, nz, units)
    near = weights(parts, 0, core, act_b, act_ext, f_all, far_act, far_cot, grad_m, cot_ext)
    far = weights(parts, 1, core, act_b, act_ext, f_all, far_act, far_cot, grad_m, cot_ext)
    far, inside = lax.optimization_barrier((far, inside))
    near = exchange(near, "x", order_x)
    far = exchange(far, "y", order_y)
    lo2, hi2 = wings(inside, act_ext, cot_ext, lo, hi, lo_far, hi_far, w1, w2)
    output, grad_s = back(act_b, lo2, hi2, grad_m, mid, sig, w1, w2)
    near, far, output, grad_s = lax.optimization_barrier((near, far, output, grad_s))
    part = jnp.stack([exchange(near, "y", order_y), exchange(far, "x", order_x)], axis=1)

    got = lax.all_to_all(part, "z", 0, 0, tiled=True)
    part = jnp.sum(got.astype(F32), axis=0).astype(BF16)
    both = lax.all_to_all(
        jnp.broadcast_to(part[None], (2 * ny,) + part.shape), ("y", "c"), 0, 0, tiled=True
    )
    both = both.reshape((ny, 2) + part.shape).astype(F32) * scale

    def assemble(layer):
        flat = both[:, layer].transpose(1, 0, 2, 3, 4).reshape(2, ny * units, 8, 128)[:, :27]
        flat = flat.reshape(2, 3, ch // 256, 3, 8, 128).transpose(1, 3, 4, 0, 2, 5)
        return flat.reshape(3, 24, ch)

    return output[None], grad_s[None], assemble(1), assemble(0)


def solution(mesh):
    fine = Mesh(mesh.devices.reshape(4, 8, 4, 2), ("x", "z", "y", "c"))
    placed = P(("y", "c"), ("x", "z"), None)
    split = P(None, ("x", "z"), None)
    return jax.shard_map(
        per_device,
        mesh=fine,
        in_specs=(placed, P(), P(), placed),
        out_specs=(placed, placed, split, split),
        check_vma=False,
    )
```

```python
import math

import jax
import jax.numpy as jnp
import numpy as np
from jax import lax
from jax.experimental import pallas as pl
from jax.experimental.pallas import tpu as pltpu
from jax.sharding import Mesh, PartitionSpec as P

FIRST = 64
SECOND = 128
CUBIC = 0.044715
ROOT = math.sqrt(2.0 / math.pi)
F32 = jnp.float32
BF16 = jnp.bfloat16


def gelu(v):
    return 0.5 * v * (1.0 + jnp.tanh(ROOT * (v + CUBIC * v * v * v)))


def gelu_both(v):
    square = v * v
    t = jnp.tanh(ROOT * v * (1.0 + CUBIC * square))
    half = 0.5 * (1.0 + t)
    slope = half + 0.5 * v * (1.0 - t * t) * (ROOT * (1.0 + 3.0 * CUBIC * square))
    return v * half, slope


def dot(a, b):
    return jnp.dot(a, b, preferred_element_type=F32)


def dot_nt(a, b):
    return lax.dot_general(a, b, (((1,), (1,)), ((), ())), preferred_element_type=F32)


def dot_tn(a, b):
    return lax.dot_general(a, b, (((0,), (0,)), ((), ())), preferred_element_type=F32)


def in_hbm(a):
    return pltpu.with_memory_space_constraint(a, pltpu.HBM)


def in_vmem(a):
    return pltpu.with_memory_space_constraint(a, pltpu.VMEM)


def edges(sig, cot):
    rows = sig.shape[0]

    def body(sig, cot, low, high, low_far, high_far, sems):
        pairs = []
        for first, last, skip_s, skip_c, take_s in (
            (low, high, 0, 0, FIRST),
            (low_far, high_far, FIRST, SECOND, SECOND),
        ):
            take_c = FIRST + SECOND - take_s
            pairs += [
                (sig, skip_s, first, 0, take_s),
                (cot, skip_c, first, take_s, take_c),
                (sig, rows - skip_s - take_s, last, 0, take_s),
                (cot, rows - skip_c - take_c, last, take_s, take_c),
            ]
        copies = [
            pltpu.make_async_copy(src.at[pl.ds(a, n)], dst.at[pl.ds(b, n)], sems.at[i])
            for i, (src, a, dst, b, n) in enumerate(pairs)
        ]
        for copy in copies:
            copy.start()
        for copy in copies:
            copy.wait()

    out = pltpu.VMEM((FIRST + SECOND, sig.shape[1]), BF16)
    return pl.pallas_call(
        body,
        in_specs=[pl.BlockSpec(memory_space=pl.ANY)] * 2,
        out_specs=[pl.BlockSpec(memory_space=pltpu.VMEM)] * 4,
        out_shape=[out] * 4,
        scratch_shapes=[pltpu.SemaphoreType.DMA((8,))],
        compiler_params=pltpu.CompilerParams(vmem_limit_bytes=2 << 20),
        name="edges",
    )(in_hbm(sig), in_hbm(cot))


def once(a):
    return pl.BlockSpec(a.shape, lambda n: (0, 0), pipeline_mode=pl.Buffered(1))


def three_taps(dots, left, weight, starts, rows):
    total = dots(left[starts[0] : starts[0] + rows], weight[0])
    for k in (1, 2):
        total = total + dots(left[starts[k] : starts[k] + rows], weight[k])
    return total


def front_kernel(core, act, cot_ext, sig, cot, w1, w2, middle, act_b, grad_m, swap, fwd, bwd):
    rows = sig.shape[0]
    fwd[...] = three_taps(dot, act, w1, [k * FIRST for k in range(3)], rows)
    bwd[...] = three_taps(dot_nt, cot_ext, w2, [(2 - k) * SECOND for k in range(3)], rows)

    @pl.loop(0, rows // 64)
    def _(i):
        at = pl.ds(pl.multiple_of(i * 64, 64), 64)
        mid = (sig[at].astype(F32) + fwd[at]).astype(BF16)
        middle[at] = mid
        value, slope = gelu_both(mid.astype(F32))
        grad = cot[at].astype(F32) + slope * bwd[at]
        act_b[at] = value.astype(BF16)
        grad_m[at] = grad.astype(BF16)
        swap[at] = jnp.where(core[0] == 0, grad, value).astype(BF16)


def front(core, act_ext, cot_ext, sig, cot, w1, w2):
    rows, ch = sig.shape
    tile = 256
    cols = pl.BlockSpec((rows, tile), lambda n: (0, n))
    out = jax.ShapeDtypeStruct((rows, ch), BF16)
    return pl.pallas_call(
        front_kernel,
        grid=(ch // tile,),
        in_specs=[
            pl.BlockSpec(memory_space=pltpu.SMEM),
            once(act_ext),
            once(cot_ext),
            cols,
            cols,
            pl.BlockSpec((3, ch, tile), lambda n: (0, 0, n)),
            pl.BlockSpec((3, tile, ch), lambda n: (0, n, 0)),
        ],
        out_specs=[cols] * 4,
        out_shape=[out] * 4,
        scratch_shapes=[pltpu.VMEM((rows, tile), F32), pltpu.VMEM((rows, tile), F32)],
        compiler_params=pltpu.CompilerParams(vmem_limit_bytes=16 << 20),
        cost_estimate=pl.CostEstimate(
            flops=12 * rows * ch * ch, transcendentals=rows * ch, bytes_accessed=14 * ch * ch
        ),
        name="front",
    )(core, act_ext, cot_ext, sig, cot, in_hbm(w1), in_hbm(w2))


def wing_kernel(inside, act, cot_ext, lo, hi, lo_far, hi_far, sig_t, cot_t, w1, w2, low, high, a_ext, c_ext):
    rows = act.shape[0] - 2 * FIRST

    @pl.when(pl.program_id(0) == 0)
    def _():
        far_low = gelu(lo_far[0:SECOND].astype(F32)).astype(BF16)
        far_high = gelu(hi_far[0:SECOND].astype(F32)).astype(BF16)
        a_ext[0, 0:SECOND] = far_low
        a_ext[0, SECOND:] = act[rows : rows + SECOND]
        a_ext[1, 0:FIRST] = far_low[FIRST:]
        a_ext[1, FIRST:SECOND] = act[0:FIRST]
        a_ext[1, SECOND : SECOND + FIRST] = act[rows + FIRST : rows + SECOND]
        a_ext[1, SECOND + FIRST :] = far_high[0:FIRST]
        a_ext[2, 0:SECOND] = act[0:SECOND]
        a_ext[2, SECOND:] = far_high
        c_ext[2, 0:FIRST] = lo_far[SECOND:]
        c_ext[2, FIRST:] = cot_ext[rows : rows + FIRST]
        c_ext[1, 0:FIRST] = cot_ext[FIRST:SECOND]
        c_ext[1, FIRST:] = cot_ext[rows + SECOND : rows + SECOND + FIRST]
        c_ext[0, 0:FIRST] = cot_ext[SECOND + FIRST : 2 * SECOND]
        c_ext[0, FIRST:] = hi_far[SECOND:]

    total = dot(a_ext[0], w1[0])
    for k in (1, 2):
        total = total + dot(a_ext[k], w1[k])
    mid = (sig_t[...].astype(F32) + total).astype(BF16).astype(F32)
    value, slope = gelu_both(mid)
    total = dot_nt(c_ext[0], w2[0])
    for k in (1, 2):
        total = total + dot_nt(c_ext[k], w2[k])
    slope = slope[SECOND - FIRST : SECOND + FIRST]
    grad = cot_t[...].astype(F32) + slope * total
    low[0:SECOND] = jnp.where(inside[0] > 0, value[0:SECOND], 0.0).astype(BF16)
    low[SECOND:] = jnp.where(inside[0] > 0, grad[0:FIRST], 0.0).astype(BF16)
    high[0:SECOND] = jnp.where(inside[1] > 0, value[SECOND:], 0.0).astype(BF16)
    high[SECOND:] = jnp.where(inside[1] > 0, grad[FIRST:], 0.0).astype(BF16)


def wings(inside, act_ext, cot_ext, lo, hi, lo_far, hi_far, w1, w2):
    ch = act_ext.shape[1]
    tile = 256
    size = FIRST + SECOND
    sig_t = jnp.concatenate([lo_far[FIRST:SECOND], lo[:FIRST], hi[:FIRST], hi_far[: SECOND - FIRST]])
    cot_t = jnp.concatenate([lo[FIRST + SECOND - FIRST :], hi[FIRST : 2 * FIRST]])
    cols = lambda a: pl.BlockSpec((a.shape[0], tile), lambda n: (0, n))
    out = jax.ShapeDtypeStruct((size, ch), BF16)
    return pl.pallas_call(
        wing_kernel,
        grid=(ch // tile,),
        in_specs=[
            pl.BlockSpec(memory_space=pltpu.SMEM),
            *[once(a) for a in (act_ext, cot_ext, lo, hi, lo_far, hi_far)],
            cols(sig_t),
            cols(cot_t),
            pl.BlockSpec((3, ch, tile), lambda n: (0, 0, n)),
            pl.BlockSpec((3, tile, ch), lambda n: (0, n, 0)),
        ],
        out_specs=[cols(out), cols(out)],
        out_shape=[out, out],
        scratch_shapes=[
            pltpu.VMEM((3, 2 * SECOND, ch), BF16),
            pltpu.VMEM((3, 2 * FIRST, ch), BF16),
        ],
        compiler_params=pltpu.CompilerParams(vmem_limit_bytes=16 << 20),
        cost_estimate=pl.CostEstimate(
            flops=6 * (2 * SECOND + 2 * FIRST) * ch * ch,
            transcendentals=4 * SECOND * ch,
            bytes_accessed=12 * ch * ch,
        ),
        name="wings",
    )(inside, act_ext, cot_ext, lo, hi, lo_far, hi_far, sig_t, cot_t, w1, w2)


def back_kernel(act_b, lo, hi, grad_m, mid, sig, gm, w1, w2, output, grad_s, a_ext, g_ext, fwd, bwd):
    rows = mid.shape[0]

    @pl.when(pl.program_id(0) == 0)
    def _():
        a_ext[0:SECOND] = lo[0:SECOND]
        a_ext[SECOND : SECOND + rows] = act_b[...]
        a_ext[SECOND + rows :] = hi[0:SECOND]
        g_ext[0:FIRST] = lo[SECOND:]
        g_ext[FIRST : FIRST + rows] = grad_m[...]
        g_ext[FIRST + rows :] = hi[SECOND:]

    total = dot(a_ext[0:rows], w2[0])
    for k in (1, 2):
        total = total + dot(a_ext[k * SECOND : k * SECOND + rows], w2[k])
    fwd[...] = total
    total = dot_nt(g_ext[2 * FIRST : 2 * FIRST + rows], w1[0])
    for k in (1, 2):
        start = (2 - k) * FIRST
        total = total + dot_nt(g_ext[start : start + rows], w1[k])
    bwd[...] = total

    @pl.loop(0, rows // 64)
    def _(i):
        at = pl.ds(pl.multiple_of(i * 64, 64), 64)
        output[at] = (mid[at].astype(F32) + fwd[at]).astype(BF16)
        _, slope = gelu_both(sig[at].astype(F32))
        grad_s[at] = (gm[at].astype(F32) + slope * bwd[at]).astype(BF16)


def back(act_b, lo, hi, grad_m, mid, sig, w1, w2):
    rows, ch = sig.shape
    tile = 256
    cols = pl.BlockSpec((rows, tile), lambda n: (0, n))
    out = jax.ShapeDtypeStruct((rows, ch), BF16)
    return pl.pallas_call(
        back_kernel,
        grid=(ch // tile,),
        in_specs=[
            once(act_b),
            once(lo),
            once(hi),
            once(grad_m),
            cols,
            cols,
            cols,
            pl.BlockSpec((3, tile, ch), lambda n: (0, n, 0)),
            pl.BlockSpec((3, ch, tile), lambda n: (0, 0, n)),
        ],
        out_specs=[cols, cols],
        out_shape=[out, out],
        scratch_shapes=[
            pltpu.VMEM((rows + 2 * SECOND, ch), BF16),
            pltpu.VMEM((rows + 2 * FIRST, ch), BF16),
            pltpu.VMEM((rows, tile), F32),
            pltpu.VMEM((rows, tile), F32),
        ],
        compiler_params=pltpu.CompilerParams(vmem_limit_bytes=16 << 20),
        cost_estimate=pl.CostEstimate(
            flops=12 * rows * ch * ch, transcendentals=rows * ch, bytes_accessed=14 * ch * ch
        ),
        name="rear",
    )(act_b, lo, hi, grad_m, mid, sig, grad_m, w1, w2)


def weight_kernel(parts, core, act_b, act_ext, f_all, far_act, right_l2, far_l2, right_l1, far_l1, out):
    nx, ny, nz, units = parts
    rows = act_b.shape[0]
    tiles = right_l2.shape[1] // 128
    count = 9 * tiles

    def emit(left_own, left_far, right_own, right_far, left_at, right_at, lead_x):
        for k in range(3):
            a, b = left_at(k), right_at(k)
            total = dot_tn(left_own[a : a + rows], right_own[b : b + rows])
            total = total + dot_tn(left_far[a : a + rows], right_far[b : b + rows])
            for j in range(tiles):
                tile = total[:, j * 128 : (j + 1) * 128].astype(BF16).reshape(nx, nz, 3, 8, 128)
                for g in range(3):
                    unit = (k * tiles + j) * 3 + g
                    y, i = unit // units, unit % units
                    if lead_x:
                        out[:, y, :, i] = tile[:, :, g]
                    else:
                        out[y, :, :, i] = tile[:, :, g]
        for unit in range(count, ny * units):
            y, i = unit // units, unit % units
            blank = jnp.zeros((nx, nz, 8, 128), BF16)
            if lead_x:
                out[:, y, :, i] = blank
            else:
                out[y, :, :, i] = blank

    @pl.when(core[0] == 0)
    def _():
        emit(act_b, f_all, right_l2, far_l2, lambda k: 0, lambda k: (2 - k) * SECOND, True)

    @pl.when(core[0] != 0)
    def _():
        emit(act_ext, far_act, right_l1, far_l1, lambda k: k * FIRST, lambda k: 0, False)


def weights(parts, start, width, core, act_b, act_ext, f_all, far_act, far_cot, grad_m, cot_ext):
    rows, ch = act_b.shape
    nx, ny, nz, units = parts
    cols = lambda a: pl.BlockSpec(
        (a.shape[0], width), lambda n: (0, start // width), pipeline_mode=pl.Buffered(1)
    )
    shape = (nx, ny, nz, units, 8, 128)
    return pl.pallas_call(
        lambda *refs: weight_kernel(parts, *refs),
        grid=(1,),
        in_specs=[
            pl.BlockSpec(memory_space=pltpu.SMEM),
            once(act_b),
            once(act_ext),
            once(f_all),
            once(far_act),
            cols(cot_ext),
            cols(far_cot),
            cols(grad_m),
            cols(f_all),
        ],
        out_specs=pl.BlockSpec(shape, lambda n: (0,) * 6),
        out_shape=pltpu.VMEM(shape, BF16),
        compiler_params=pltpu.CompilerParams(vmem_limit_bytes=20 << 20),
        cost_estimate=pl.CostEstimate(
            flops=12 * rows * ch * width, transcendentals=0, bytes_accessed=12 * ch * width
        ),
        name="weights",
    )(core, act_b, act_ext, f_all, far_act, cot_ext, far_cot, grad_m, f_all)


def exchange(data, order, core_axis):
    axes = ("x", "z", "y", "c")
    sizes = [lax.axis_size(a) for a in axes]
    n = data.shape[0]
    rest = data.shape[1:]

    def pairs(k):
        found = []
        for i in range(math.prod(sizes)):
            place = list(np.unravel_index(i, sizes))
            at = axes.index(core_axis[place[3]])
            place[at] = (place[at] + k) % n
            found.append((i, int(np.ravel_multi_index(place, sizes))))
        return found

    total = None
    for k in (0, 1, n - 1, *range(2, n - 1)):
        chunk = lax.dynamic_slice(
            data, (order[k],) + (0,) * len(rest), (1,) + rest, allow_negative_indices=False
        ).reshape(rest)
        if k:
            chunk = lax.ppermute(chunk, axes, pairs(k))
        chunk = chunk.astype(F32)
        total = chunk if total is None else total + chunk
    return total.astype(BF16)


def order_of(me, n):
    return [jnp.where(me + k < n, me + k, me + k - n) for k in range(n)]


def neighbours(low, high):
    axes = ("x", "z")
    count = lax.axis_size("x") * lax.axis_size("z")
    forward = [(i, i + 1) for i in range(count - 1)]
    backward = [(t, s) for s, t in forward]
    return lax.ppermute(high, axes, forward), lax.ppermute(low, axes, backward)


def per_device(signal, w1, w2, cotangent):
    sig, cot = signal[0], cotangent[0]
    rows, ch = sig.shape
    nx, ny, nz = (lax.axis_size(a) for a in ("x", "y", "z"))
    tokens = signal.shape[0] * ny * lax.axis_size("c") * rows * nx * nz
    scale = 1.0 / math.sqrt(tokens)
    splits = [(0, 512), (512, 256)]
    sizes = [9 * width // 128 for _, width in splits]
    units = [-(-size // ny) for size in sizes]
    core = lax.axis_index("c").astype(jnp.int32).reshape(1)
    place = lax.axis_index("x") * nz + lax.axis_index("z")
    inside = jnp.stack([place > 0, place < nx * nz - 1]).astype(jnp.int32)

    at_x, at_y = (lax.axis_index(a).astype(jnp.int32) for a in ("x", "y"))
    order_a = order_of(jnp.where(core[0] == 0, at_x, at_y), nx)
    order_b = order_of(jnp.where(core[0] == 0, at_y, at_x), ny)
    sig, cot, core, inside, order_a, order_b = lax.optimization_barrier(
        (sig, cot, core, inside, order_a, order_b)
    )

    low, high, low_far, high_far = edges(sig, cot)
    lo, hi = neighbours(low, high)
    lo_far, hi_far = neighbours(low_far, high_far)
    act = lambda v: gelu(v.astype(F32)).astype(BF16)
    act_ext = jnp.concatenate([act(lo[:FIRST]), act(sig), act(hi[:FIRST])])
    cot_ext = jnp.concatenate([lo[FIRST:], cot, hi[FIRST:]])
    swap = lambda a: lax.ppermute(a, "c", [(0, 1), (1, 0)])
    far_act, far_cot = swap(act_ext), swap(cot_ext)
    mid, act_b, grad_m, give = front(core, act_ext, cot_ext, sig, cot, w1, w2)
    f_all = swap(give)
    pieces = [
        weights((nx, ny, nz, u), *split, core, act_b, act_ext, f_all, far_act, far_cot, grad_m, cot_ext)
        for split, u in zip(splits, units)
    ]
    pieces[-1], inside = lax.optimization_barrier((pieces[-1], inside))
    pieces = [exchange(piece, order_a, "xy") for piece in pieces]
    lo2, hi2 = wings(inside, act_ext, cot_ext, lo, hi, lo_far, hi_far, w1, w2)
    output, grad_s = back(act_b, lo2, hi2, grad_m, mid, sig, w1, w2)
    pieces, output, grad_s = lax.optimization_barrier((pieces, output, grad_s))
    part = exchange(jnp.concatenate(pieces, axis=2), order_b, "yx")

    got = lax.all_to_all(part, "z", 0, 0, tiled=True)
    part = jnp.sum(got.astype(F32), axis=0).astype(BF16)
    both = lax.all_to_all(
        jnp.broadcast_to(part[None], (2 * ny,) + part.shape), ("y", "c"), 0, 0, tiled=True
    )
    both = both.reshape((ny, 2) + part.shape).astype(F32) * scale

    def assemble(layer):
        found, at = [], 0
        for (_, width), size, u in zip(splits, sizes, units):
            flat = both[:, layer, at : at + u].reshape(ny * u, 8, 128)[:size]
            flat = flat.reshape(3, width // 128, 3, 8, 128).transpose(0, 2, 3, 1, 4)
            found.append(flat.reshape(3, 24, width))
            at += u
        return jnp.concatenate(found, axis=2)

    return output[None], grad_s[None], assemble(1), assemble(0)


def solution(mesh):
    fine = Mesh(mesh.devices.reshape(4, 8, 4, 2), ("x", "z", "y", "c"))
    placed = P(("y", "c"), ("x", "z"), None)
    split = P(None, ("x", "z"), None)
    return jax.shard_map(
        per_device,
        mesh=fine,
        in_specs=(placed, P(), P(), placed),
        out_specs=(placed, placed, split, split),
        check_vma=False,
    )
```

```python
import math

import jax
import jax.numpy as jnp
import numpy as np
from jax import lax
from jax.experimental import pallas as pl
from jax.experimental.pallas import tpu as pltpu
from jax.sharding import Mesh, PartitionSpec as P

FIRST = 64
SECOND = 128
CUBIC = 0.044715
ROOT = math.sqrt(2.0 / math.pi)
F32 = jnp.float32
BF16 = jnp.bfloat16


def gelu(v):
    return 0.5 * v * (1.0 + jnp.tanh(ROOT * (v + CUBIC * v * v * v)))


def gelu_both(v):
    square = v * v
    t = jnp.tanh(ROOT * v * (1.0 + CUBIC * square))
    half = 0.5 * (1.0 + t)
    slope = half + 0.5 * v * (1.0 - t * t) * (ROOT * (1.0 + 3.0 * CUBIC * square))
    return v * half, slope


def dot(a, b):
    return jnp.dot(a, b, preferred_element_type=F32)


def dot_nt(a, b):
    return lax.dot_general(a, b, (((1,), (1,)), ((), ())), preferred_element_type=F32)


def dot_tn(a, b):
    return lax.dot_general(a, b, (((0,), (0,)), ((), ())), preferred_element_type=F32)


def in_hbm(a):
    return pltpu.with_memory_space_constraint(a, pltpu.HBM)


def in_vmem(a):
    return pltpu.with_memory_space_constraint(a, pltpu.VMEM)


def edges(sig, cot):
    rows = sig.shape[0]

    def body(sig, cot, low, high, low_far, high_far, sems):
        pairs = []
        for first, last, skip_s, skip_c, take_s in (
            (low, high, 0, 0, FIRST),
            (low_far, high_far, FIRST, SECOND, SECOND),
        ):
            take_c = FIRST + SECOND - take_s
            pairs += [
                (sig, skip_s, first, 0, take_s),
                (cot, skip_c, first, take_s, take_c),
                (sig, rows - skip_s - take_s, last, 0, take_s),
                (cot, rows - skip_c - take_c, last, take_s, take_c),
            ]
        copies = [
            pltpu.make_async_copy(src.at[pl.ds(a, n)], dst.at[pl.ds(b, n)], sems.at[i])
            for i, (src, a, dst, b, n) in enumerate(pairs)
        ]
        for copy in copies:
            copy.start()
        for copy in copies:
            copy.wait()

    out = pltpu.VMEM((FIRST + SECOND, sig.shape[1]), BF16)
    return pl.pallas_call(
        body,
        in_specs=[pl.BlockSpec(memory_space=pl.ANY)] * 2,
        out_specs=[pl.BlockSpec(memory_space=pltpu.VMEM)] * 4,
        out_shape=[out] * 4,
        scratch_shapes=[pltpu.SemaphoreType.DMA((8,))],
        compiler_params=pltpu.CompilerParams(vmem_limit_bytes=2 << 20),
        name="edges",
    )(in_hbm(sig), in_hbm(cot))


def once(a):
    return pl.BlockSpec(a.shape, lambda n: (0, 0), pipeline_mode=pl.Buffered(1))


CHUNK = 256


def three_taps(dots, left, weight, starts, at):
    total = dots(left[starts[0] + at : starts[0] + at + CHUNK], weight[0])
    for k in (1, 2):
        total = total + dots(left[starts[k] + at : starts[k] + at + CHUNK], weight[k])
    return total


def front_kernel(core, act, cot_ext, sig, cot, w1, w2, middle, act_b, grad_m, swap):
    for i in range(0, sig.shape[0], CHUNK):
        at = slice(i, i + CHUNK)
        fwd = three_taps(dot, act, w1, [k * FIRST for k in range(3)], i)
        bwd = three_taps(dot_nt, cot_ext, w2, [(2 - k) * SECOND for k in range(3)], i)
        mid = (sig[at].astype(F32) + fwd).astype(BF16)
        middle[at] = mid
        value, slope = gelu_both(mid.astype(F32))
        grad = cot[at].astype(F32) + slope * bwd
        act_b[at] = value.astype(BF16)
        grad_m[at] = grad.astype(BF16)
        swap[at] = jnp.where(core[0] == 0, grad, value).astype(BF16)


def front(core, act_ext, cot_ext, sig, cot, w1, w2):
    rows, ch = sig.shape
    tile = 256
    cols = pl.BlockSpec((rows, tile), lambda n: (0, n))
    out = jax.ShapeDtypeStruct((rows, ch), BF16)
    return pl.pallas_call(
        front_kernel,
        grid=(ch // tile,),
        in_specs=[
            pl.BlockSpec(memory_space=pltpu.SMEM),
            once(act_ext),
            once(cot_ext),
            cols,
            cols,
            pl.BlockSpec((3, ch, tile), lambda n: (0, 0, n)),
            pl.BlockSpec((3, tile, ch), lambda n: (0, n, 0)),
        ],
        out_specs=[cols] * 4,
        out_shape=[out] * 4,
        compiler_params=pltpu.CompilerParams(vmem_limit_bytes=16 << 20),
        cost_estimate=pl.CostEstimate(
            flops=12 * rows * ch * ch, transcendentals=rows * ch, bytes_accessed=14 * ch * ch
        ),
        name="front",
    )(core, act_ext, cot_ext, sig, cot, in_hbm(w1), in_hbm(w2))


def wing_kernel(inside, act, cot_ext, lo, hi, lo_far, hi_far, sig_t, cot_t, w1, w2, low, high, a_ext, c_ext):
    rows = act.shape[0] - 2 * FIRST

    @pl.when(pl.program_id(0) == 0)
    def _():
        far_low = gelu(lo_far[0:SECOND].astype(F32)).astype(BF16)
        far_high = gelu(hi_far[0:SECOND].astype(F32)).astype(BF16)
        a_ext[0, 0:SECOND] = far_low
        a_ext[0, SECOND:] = act[rows : rows + SECOND]
        a_ext[1, 0:FIRST] = far_low[FIRST:]
        a_ext[1, FIRST:SECOND] = act[0:FIRST]
        a_ext[1, SECOND : SECOND + FIRST] = act[rows + FIRST : rows + SECOND]
        a_ext[1, SECOND + FIRST :] = far_high[0:FIRST]
        a_ext[2, 0:SECOND] = act[0:SECOND]
        a_ext[2, SECOND:] = far_high
        c_ext[2, 0:FIRST] = lo_far[SECOND:]
        c_ext[2, FIRST:] = cot_ext[rows : rows + FIRST]
        c_ext[1, 0:FIRST] = cot_ext[FIRST:SECOND]
        c_ext[1, FIRST:] = cot_ext[rows + SECOND : rows + SECOND + FIRST]
        c_ext[0, 0:FIRST] = cot_ext[SECOND + FIRST : 2 * SECOND]
        c_ext[0, FIRST:] = hi_far[SECOND:]

    total = dot(a_ext[0], w1[0])
    for k in (1, 2):
        total = total + dot(a_ext[k], w1[k])
    mid = (sig_t[...].astype(F32) + total).astype(BF16).astype(F32)
    value, slope = gelu_both(mid)
    total = dot_nt(c_ext[0], w2[0])
    for k in (1, 2):
        total = total + dot_nt(c_ext[k], w2[k])
    slope = slope[SECOND - FIRST : SECOND + FIRST]
    grad = cot_t[...].astype(F32) + slope * total
    low[0:SECOND] = jnp.where(inside[0] > 0, value[0:SECOND], 0.0).astype(BF16)
    low[SECOND:] = jnp.where(inside[0] > 0, grad[0:FIRST], 0.0).astype(BF16)
    high[0:SECOND] = jnp.where(inside[1] > 0, value[SECOND:], 0.0).astype(BF16)
    high[SECOND:] = jnp.where(inside[1] > 0, grad[FIRST:], 0.0).astype(BF16)


def wings(inside, act_ext, cot_ext, lo, hi, lo_far, hi_far, w1, w2):
    ch = act_ext.shape[1]
    tile = 256
    size = FIRST + SECOND
    sig_t = jnp.concatenate([lo_far[FIRST:SECOND], lo[:FIRST], hi[:FIRST], hi_far[: SECOND - FIRST]])
    cot_t = jnp.concatenate([lo[FIRST + SECOND - FIRST :], hi[FIRST : 2 * FIRST]])
    cols = lambda a: pl.BlockSpec((a.shape[0], tile), lambda n: (0, n))
    out = jax.ShapeDtypeStruct((size, ch), BF16)
    return pl.pallas_call(
        wing_kernel,
        grid=(ch // tile,),
        in_specs=[
            pl.BlockSpec(memory_space=pltpu.SMEM),
            *[once(a) for a in (act_ext, cot_ext, lo, hi, lo_far, hi_far)],
            cols(sig_t),
            cols(cot_t),
            pl.BlockSpec((3, ch, tile), lambda n: (0, 0, n)),
            pl.BlockSpec((3, tile, ch), lambda n: (0, n, 0)),
        ],
        out_specs=[cols(out), cols(out)],
        out_shape=[out, out],
        scratch_shapes=[
            pltpu.VMEM((3, 2 * SECOND, ch), BF16),
            pltpu.VMEM((3, 2 * FIRST, ch), BF16),
        ],
        compiler_params=pltpu.CompilerParams(vmem_limit_bytes=16 << 20),
        cost_estimate=pl.CostEstimate(
            flops=6 * (2 * SECOND + 2 * FIRST) * ch * ch,
            transcendentals=4 * SECOND * ch,
            bytes_accessed=12 * ch * ch,
        ),
        name="wings",
    )(inside, act_ext, cot_ext, lo, hi, lo_far, hi_far, sig_t, cot_t, w1, w2)


def back_kernel(act_b, lo, hi, grad_m, mid, sig, gm, w1, w2, output, grad_s, a_ext, g_ext):
    rows = mid.shape[0]

    @pl.when(pl.program_id(0) == 0)
    def _():
        a_ext[0:SECOND] = lo[0:SECOND]
        a_ext[SECOND : SECOND + rows] = act_b[...]
        a_ext[SECOND + rows :] = hi[0:SECOND]
        g_ext[0:FIRST] = lo[SECOND:]
        g_ext[FIRST : FIRST + rows] = grad_m[...]
        g_ext[FIRST + rows :] = hi[SECOND:]

    for i in range(0, rows, CHUNK):
        at = slice(i, i + CHUNK)
        fwd = three_taps(dot, a_ext, w2, [k * SECOND for k in range(3)], i)
        bwd = three_taps(dot_nt, g_ext, w1, [(2 - k) * FIRST for k in range(3)], i)
        output[at] = (mid[at].astype(F32) + fwd).astype(BF16)
        _, slope = gelu_both(sig[at].astype(F32))
        grad_s[at] = (gm[at].astype(F32) + slope * bwd).astype(BF16)


def back(act_b, lo, hi, grad_m, mid, sig, w1, w2):
    rows, ch = sig.shape
    tile = 256
    cols = pl.BlockSpec((rows, tile), lambda n: (0, n))
    out = jax.ShapeDtypeStruct((rows, ch), BF16)
    return pl.pallas_call(
        back_kernel,
        grid=(ch // tile,),
        in_specs=[
            once(act_b),
            once(lo),
            once(hi),
            once(grad_m),
            cols,
            cols,
            cols,
            pl.BlockSpec((3, tile, ch), lambda n: (0, n, 0)),
            pl.BlockSpec((3, ch, tile), lambda n: (0, 0, n)),
        ],
        out_specs=[cols, cols],
        out_shape=[out, out],
        scratch_shapes=[
            pltpu.VMEM((rows + 2 * SECOND, ch), BF16),
            pltpu.VMEM((rows + 2 * FIRST, ch), BF16),
        ],
        compiler_params=pltpu.CompilerParams(vmem_limit_bytes=16 << 20),
        cost_estimate=pl.CostEstimate(
            flops=12 * rows * ch * ch, transcendentals=rows * ch, bytes_accessed=14 * ch * ch
        ),
        name="rear",
    )(act_b, lo, hi, grad_m, mid, sig, grad_m, w1, w2)


def weight_kernel(parts, core, act_b, act_ext, f_all, far_act, right_l2, far_l2, right_l1, far_l1, out):
    nx, ny, nz, units = parts
    rows = act_b.shape[0]
    tiles = right_l2.shape[1] // 128
    count = 9 * tiles

    def emit(left_own, left_far, right_own, right_far, left_at, right_at, lead_x):
        for k in range(3):
            a, b = left_at(k), right_at(k)
            total = dot_tn(left_own[a : a + rows], right_own[b : b + rows])
            total = total + dot_tn(left_far[a : a + rows], right_far[b : b + rows])
            for j in range(tiles):
                tile = total[:, j * 128 : (j + 1) * 128].astype(BF16).reshape(nx, nz, 3, 8, 128)
                for g in range(3):
                    unit = (k * tiles + j) * 3 + g
                    y, i = unit // units, unit % units
                    if lead_x:
                        out[:, y, :, i] = tile[:, :, g]
                    else:
                        out[y, :, :, i] = tile[:, :, g]
        for unit in range(count, ny * units):
            y, i = unit // units, unit % units
            blank = jnp.zeros((nx, nz, 8, 128), BF16)
            if lead_x:
                out[:, y, :, i] = blank
            else:
                out[y, :, :, i] = blank

    @pl.when(core[0] == 0)
    def _():
        emit(act_b, f_all, right_l2, far_l2, lambda k: 0, lambda k: (2 - k) * SECOND, True)

    @pl.when(core[0] != 0)
    def _():
        emit(act_ext, far_act, right_l1, far_l1, lambda k: k * FIRST, lambda k: 0, False)


def weights(parts, start, width, core, act_b, act_ext, f_all, far_act, far_cot, grad_m, cot_ext):
    rows, ch = act_b.shape
    nx, ny, nz, units = parts
    cols = lambda a: pl.BlockSpec(
        (a.shape[0], width), lambda n: (0, start // width), pipeline_mode=pl.Buffered(1)
    )
    shape = (nx, ny, nz, units, 8, 128)
    return pl.pallas_call(
        lambda *refs: weight_kernel(parts, *refs),
        grid=(1,),
        in_specs=[
            pl.BlockSpec(memory_space=pltpu.SMEM),
            once(act_b),
            once(act_ext),
            once(f_all),
            once(far_act),
            cols(cot_ext),
            cols(far_cot),
            cols(grad_m),
            cols(f_all),
        ],
        out_specs=pl.BlockSpec(shape, lambda n: (0,) * 6),
        out_shape=pltpu.VMEM(shape, BF16),
        compiler_params=pltpu.CompilerParams(vmem_limit_bytes=20 << 20),
        cost_estimate=pl.CostEstimate(
            flops=12 * rows * ch * width, transcendentals=0, bytes_accessed=12 * ch * width
        ),
        name="weights",
    )(core, act_b, act_ext, f_all, far_act, cot_ext, far_cot, grad_m, f_all)


def exchange(data, order, core_axis, token=None):
    axes = ("x", "z", "y", "c")
    sizes = [lax.axis_size(a) for a in axes]
    n = data.shape[0]
    rest = data.shape[1:]

    def pairs(k):
        found = []
        for i in range(math.prod(sizes)):
            place = list(np.unravel_index(i, sizes))
            at = axes.index(core_axis[place[3]])
            place[at] = (place[at] + k) % n
            found.append((i, int(np.ravel_multi_index(place, sizes))))
        return found

    total = None
    for k in (0, *range(2, n - 1), 1, n - 1):
        chunk = lax.dynamic_slice(
            data, (order[k],) + (0,) * len(rest), (1,) + rest, allow_negative_indices=False
        ).reshape(rest)
        if k:
            chunk = lax.ppermute(chunk, axes, pairs(k))
        if k == 2 and token is not None:
            chunk, token = lax.optimization_barrier((chunk, token))
        chunk = chunk.astype(F32)
        total = chunk if total is None else total + chunk
    return total.astype(BF16), token


def order_of(me, n):
    return [jnp.where(me + k < n, me + k, me + k - n) for k in range(n)]


def neighbours(low, high):
    axes = ("x", "z")
    count = lax.axis_size("x") * lax.axis_size("z")
    forward = [(i, i + 1) for i in range(count - 1)]
    backward = [(t, s) for s, t in forward]
    return lax.ppermute(high, axes, forward), lax.ppermute(low, axes, backward)


def per_device(signal, w1, w2, cotangent):
    sig, cot = signal[0], cotangent[0]
    rows, ch = sig.shape
    nx, ny, nz = (lax.axis_size(a) for a in ("x", "y", "z"))
    tokens = signal.shape[0] * ny * lax.axis_size("c") * rows * nx * nz
    scale = 1.0 / math.sqrt(tokens)
    splits = [(0, 512), (512, 256)]
    sizes = [9 * width // 128 for _, width in splits]
    units = [-(-size // ny) for size in sizes]
    core = lax.axis_index("c").astype(jnp.int32).reshape(1)
    place = lax.axis_index("x") * nz + lax.axis_index("z")
    inside = jnp.stack([place > 0, place < nx * nz - 1]).astype(jnp.int32)

    at_x, at_y = (lax.axis_index(a).astype(jnp.int32) for a in ("x", "y"))
    order_a = order_of(jnp.where(core[0] == 0, at_x, at_y), nx)
    order_b = order_of(jnp.where(core[0] == 0, at_y, at_x), ny)
    sig, cot, core, inside, order_a, order_b = lax.optimization_barrier(
        (sig, cot, core, inside, order_a, order_b)
    )

    low, high, low_far, high_far = edges(sig, cot)
    lo, hi = neighbours(low, high)
    lo_far, hi_far = neighbours(low_far, high_far)
    act = lambda v: gelu(v.astype(F32)).astype(BF16)
    act_ext = jnp.concatenate([act(lo[:FIRST]), act(sig), act(hi[:FIRST])])
    cot_ext = jnp.concatenate([lo[FIRST:], cot, hi[FIRST:]])
    swap = lambda a: lax.ppermute(a, "c", [(0, 1), (1, 0)])
    far_act, far_cot = swap(act_ext), swap(cot_ext)
    mid, act_b, grad_m, give = front(core, act_ext, cot_ext, sig, cot, w1, w2)
    f_all = swap(give)
    pieces = [
        weights((nx, ny, nz, u), *split, core, act_b, act_ext, f_all, far_act, far_cot, grad_m, cot_ext)
        for split, u in zip(splits, units)
    ]
    wide, _ = exchange(pieces[0], order_a, "xy")
    narrow, inside = exchange(pieces[1], order_a, "xy", inside)
    pieces = [wide, narrow]
    lo2, hi2 = wings(inside, act_ext, cot_ext, lo, hi, lo_far, hi_far, w1, w2)
    output, grad_s = back(act_b, lo2, hi2, grad_m, mid, sig, w1, w2)
    pieces, output, grad_s = lax.optimization_barrier((pieces, output, grad_s))
    part, _ = exchange(jnp.concatenate(pieces, axis=2), order_b, "yx")

    got = lax.all_to_all(part, "z", 0, 0, tiled=True)
    part = jnp.sum(got.astype(F32), axis=0).astype(BF16)
    both = lax.all_to_all(
        jnp.broadcast_to(part[None], (2 * ny,) + part.shape), ("y", "c"), 0, 0, tiled=True
    )
    both = both.reshape((ny, 2) + part.shape).astype(F32) * scale

    def assemble(layer):
        found, at = [], 0
        for (_, width), size, u in zip(splits, sizes, units):
            flat = both[:, layer, at : at + u].reshape(ny * u, 8, 128)[:size]
            flat = flat.reshape(3, width // 128, 3, 8, 128).transpose(0, 2, 3, 1, 4)
            found.append(flat.reshape(3, 24, width))
            at += u
        return jnp.concatenate(found, axis=2)

    return output[None], grad_s[None], assemble(1), assemble(0)


def solution(mesh):
    fine = Mesh(mesh.devices.reshape(4, 8, 4, 2), ("x", "z", "y", "c"))
    placed = P(("y", "c"), ("x", "z"), None)
    split = P(None, ("x", "z"), None)
    return jax.shard_map(
        per_device,
        mesh=fine,
        in_specs=(placed, P(), P(), placed),
        out_specs=(placed, placed, split, split),
        check_vma=False,
    )
```

```python
import math

import jax
import jax.numpy as jnp
import numpy as np
from jax import lax
from jax.experimental import pallas as pl
from jax.experimental.pallas import tpu as pltpu
from jax.sharding import Mesh, PartitionSpec as P

FIRST = 64
SECOND = 128
CUBIC = 0.044715
ROOT = math.sqrt(2.0 / math.pi)
F32 = jnp.float32
BF16 = jnp.bfloat16


def gelu(v):
    return 0.5 * v * (1.0 + jnp.tanh(ROOT * (v + CUBIC * v * v * v)))


def gelu_both(v):
    square = v * v
    t = jnp.tanh(ROOT * v * (1.0 + CUBIC * square))
    half = 0.5 * (1.0 + t)
    slope = half + 0.5 * v * (1.0 - t * t) * (ROOT * (1.0 + 3.0 * CUBIC * square))
    return v * half, slope


def dot(a, b):
    return jnp.dot(a, b, preferred_element_type=F32)


def dot_nt(a, b):
    return lax.dot_general(a, b, (((1,), (1,)), ((), ())), preferred_element_type=F32)


def dot_tn(a, b):
    return lax.dot_general(a, b, (((0,), (0,)), ((), ())), preferred_element_type=F32)


def in_hbm(a):
    return pltpu.with_memory_space_constraint(a, pltpu.HBM)


def in_vmem(a):
    return pltpu.with_memory_space_constraint(a, pltpu.VMEM)


def edges(sig, cot):
    rows = sig.shape[0]

    def body(sig, cot, low, high, low_far, high_far, sems):
        pairs = []
        for first, last, skip_s, skip_c, take_s in (
            (low, high, 0, 0, FIRST),
            (low_far, high_far, FIRST, SECOND, SECOND),
        ):
            take_c = FIRST + SECOND - take_s
            pairs += [
                (sig, skip_s, first, 0, take_s),
                (cot, skip_c, first, take_s, take_c),
                (sig, rows - skip_s - take_s, last, 0, take_s),
                (cot, rows - skip_c - take_c, last, take_s, take_c),
            ]
        copies = [
            pltpu.make_async_copy(src.at[pl.ds(a, n)], dst.at[pl.ds(b, n)], sems.at[i])
            for i, (src, a, dst, b, n) in enumerate(pairs)
        ]
        for copy in copies:
            copy.start()
        for copy in copies:
            copy.wait()

    out = pltpu.VMEM((FIRST + SECOND, sig.shape[1]), BF16)
    return pl.pallas_call(
        body,
        in_specs=[pl.BlockSpec(memory_space=pl.ANY)] * 2,
        out_specs=[pl.BlockSpec(memory_space=pltpu.VMEM)] * 4,
        out_shape=[out] * 4,
        scratch_shapes=[pltpu.SemaphoreType.DMA((8,))],
        compiler_params=pltpu.CompilerParams(vmem_limit_bytes=2 << 20),
        name="edges",
    )(in_hbm(sig), in_hbm(cot))


def once(a):
    return pl.BlockSpec(a.shape, lambda n: (0, 0), pipeline_mode=pl.Buffered(1))


CHUNK = 256


def three_taps(dots, left, weight, starts, at):
    total = dots(left[starts[0] + at : starts[0] + at + CHUNK], weight[0])
    for k in (1, 2):
        total = total + dots(left[starts[k] + at : starts[k] + at + CHUNK], weight[k])
    return total


def front_kernel(core, act, cot_ext, sig, cot, w1, w2, middle, act_b, grad_m, swap):
    for i in range(0, sig.shape[0], CHUNK):
        at = slice(i, i + CHUNK)
        fwd = three_taps(dot, act, w1, [k * FIRST for k in range(3)], i)
        bwd = three_taps(dot_nt, cot_ext, w2, [(2 - k) * SECOND for k in range(3)], i)
        mid = (sig[at].astype(F32) + fwd).astype(BF16)
        middle[at] = mid
        value, slope = gelu_both(mid.astype(F32))
        grad = cot[at].astype(F32) + slope * bwd
        act_b[at] = value.astype(BF16)
        grad_m[at] = grad.astype(BF16)
        swap[at] = jnp.where(core[0] == 0, grad, value).astype(BF16)


def front(core, act_ext, cot_ext, sig, cot, w1, w2):
    rows, ch = sig.shape
    tile = 256
    cols = pl.BlockSpec((rows, tile), lambda n: (0, n))
    out = jax.ShapeDtypeStruct((rows, ch), BF16)
    return pl.pallas_call(
        front_kernel,
        grid=(ch // tile,),
        in_specs=[
            pl.BlockSpec(memory_space=pltpu.SMEM),
            once(act_ext),
            once(cot_ext),
            cols,
            cols,
            pl.BlockSpec((3, ch, tile), lambda n: (0, 0, n)),
            pl.BlockSpec((3, tile, ch), lambda n: (0, n, 0)),
        ],
        out_specs=[cols] * 4,
        out_shape=[out] * 4,
        compiler_params=pltpu.CompilerParams(vmem_limit_bytes=16 << 20),
        cost_estimate=pl.CostEstimate(
            flops=12 * rows * ch * ch, transcendentals=rows * ch, bytes_accessed=14 * ch * ch
        ),
        name="front",
    )(core, act_ext, cot_ext, sig, cot, in_hbm(w1), in_hbm(w2))


def wing_kernel(inside, act, cot_ext, lo, hi, lo_far, hi_far, sig_t, cot_t, w1, w2, low, high, a_ext, c_ext):
    rows = act.shape[0] - 2 * FIRST

    @pl.when(pl.program_id(0) == 0)
    def _():
        far_low = gelu(lo_far[0:SECOND].astype(F32)).astype(BF16)
        far_high = gelu(hi_far[0:SECOND].astype(F32)).astype(BF16)
        a_ext[0, 0:SECOND] = far_low
        a_ext[0, SECOND:] = act[rows : rows + SECOND]
        a_ext[1, 0:FIRST] = far_low[FIRST:]
        a_ext[1, FIRST:SECOND] = act[0:FIRST]
        a_ext[1, SECOND : SECOND + FIRST] = act[rows + FIRST : rows + SECOND]
        a_ext[1, SECOND + FIRST :] = far_high[0:FIRST]
        a_ext[2, 0:SECOND] = act[0:SECOND]
        a_ext[2, SECOND:] = far_high
        c_ext[2, 0:FIRST] = lo_far[SECOND:]
        c_ext[2, FIRST:] = cot_ext[rows : rows + FIRST]
        c_ext[1, 0:FIRST] = cot_ext[FIRST:SECOND]
        c_ext[1, FIRST:] = cot_ext[rows + SECOND : rows + SECOND + FIRST]
        c_ext[0, 0:FIRST] = cot_ext[SECOND + FIRST : 2 * SECOND]
        c_ext[0, FIRST:] = hi_far[SECOND:]

    total = dot(a_ext[0], w1[0])
    for k in (1, 2):
        total = total + dot(a_ext[k], w1[k])
    mid = (sig_t[...].astype(F32) + total).astype(BF16).astype(F32)
    value, slope = gelu_both(mid)
    total = dot_nt(c_ext[0], w2[0])
    for k in (1, 2):
        total = total + dot_nt(c_ext[k], w2[k])
    slope = slope[SECOND - FIRST : SECOND + FIRST]
    grad = cot_t[...].astype(F32) + slope * total
    low[0:SECOND] = jnp.where(inside[0] > 0, value[0:SECOND], 0.0).astype(BF16)
    low[SECOND:] = jnp.where(inside[0] > 0, grad[0:FIRST], 0.0).astype(BF16)
    high[0:SECOND] = jnp.where(inside[1] > 0, value[SECOND:], 0.0).astype(BF16)
    high[SECOND:] = jnp.where(inside[1] > 0, grad[FIRST:], 0.0).astype(BF16)


def wings(inside, act_ext, cot_ext, lo, hi, lo_far, hi_far, w1, w2):
    ch = act_ext.shape[1]
    tile = 256
    size = FIRST + SECOND
    sig_t = jnp.concatenate([lo_far[FIRST:SECOND], lo[:FIRST], hi[:FIRST], hi_far[: SECOND - FIRST]])
    cot_t = jnp.concatenate([lo[FIRST + SECOND - FIRST :], hi[FIRST : 2 * FIRST]])
    cols = lambda a: pl.BlockSpec((a.shape[0], tile), lambda n: (0, n))
    out = jax.ShapeDtypeStruct((size, ch), BF16)
    return pl.pallas_call(
        wing_kernel,
        grid=(ch // tile,),
        in_specs=[
            pl.BlockSpec(memory_space=pltpu.SMEM),
            *[once(a) for a in (act_ext, cot_ext, lo, hi, lo_far, hi_far)],
            cols(sig_t),
            cols(cot_t),
            pl.BlockSpec((3, ch, tile), lambda n: (0, 0, n)),
            pl.BlockSpec((3, tile, ch), lambda n: (0, n, 0)),
        ],
        out_specs=[cols(out), cols(out)],
        out_shape=[out, out],
        scratch_shapes=[
            pltpu.VMEM((3, 2 * SECOND, ch), BF16),
            pltpu.VMEM((3, 2 * FIRST, ch), BF16),
        ],
        compiler_params=pltpu.CompilerParams(vmem_limit_bytes=16 << 20),
        cost_estimate=pl.CostEstimate(
            flops=6 * (2 * SECOND + 2 * FIRST) * ch * ch,
            transcendentals=4 * SECOND * ch,
            bytes_accessed=12 * ch * ch,
        ),
        name="wings",
    )(inside, act_ext, cot_ext, lo, hi, lo_far, hi_far, sig_t, cot_t, w1, w2)


def back_kernel(act_b, lo, hi, grad_m, mid, sig, gm, w1, w2, output, grad_s, a_ext, g_ext):
    rows = mid.shape[0]

    @pl.when(pl.program_id(0) == 0)
    def _():
        a_ext[0:SECOND] = lo[0:SECOND]
        a_ext[SECOND : SECOND + rows] = act_b[...]
        a_ext[SECOND + rows :] = hi[0:SECOND]
        g_ext[0:FIRST] = lo[SECOND:]
        g_ext[FIRST : FIRST + rows] = grad_m[...]
        g_ext[FIRST + rows :] = hi[SECOND:]

    for i in range(0, rows, CHUNK):
        at = slice(i, i + CHUNK)
        fwd = three_taps(dot, a_ext, w2, [k * SECOND for k in range(3)], i)
        bwd = three_taps(dot_nt, g_ext, w1, [(2 - k) * FIRST for k in range(3)], i)
        output[at] = (mid[at].astype(F32) + fwd).astype(BF16)
        _, slope = gelu_both(sig[at].astype(F32))
        grad_s[at] = (gm[at].astype(F32) + slope * bwd).astype(BF16)


def back(act_b, lo, hi, grad_m, mid, sig, w1, w2):
    rows, ch = sig.shape
    tile = 256
    cols = pl.BlockSpec((rows, tile), lambda n: (0, n))
    out = jax.ShapeDtypeStruct((rows, ch), BF16)
    return pl.pallas_call(
        back_kernel,
        grid=(ch // tile,),
        in_specs=[
            once(act_b),
            once(lo),
            once(hi),
            once(grad_m),
            cols,
            cols,
            cols,
            pl.BlockSpec((3, tile, ch), lambda n: (0, n, 0)),
            pl.BlockSpec((3, ch, tile), lambda n: (0, 0, n)),
        ],
        out_specs=[cols, cols],
        out_shape=[out, out],
        scratch_shapes=[
            pltpu.VMEM((rows + 2 * SECOND, ch), BF16),
            pltpu.VMEM((rows + 2 * FIRST, ch), BF16),
        ],
        compiler_params=pltpu.CompilerParams(vmem_limit_bytes=16 << 20),
        cost_estimate=pl.CostEstimate(
            flops=12 * rows * ch * ch, transcendentals=rows * ch, bytes_accessed=14 * ch * ch
        ),
        name="rear",
    )(act_b, lo, hi, grad_m, mid, sig, grad_m, w1, w2)


def weight_kernel(parts, core, act_b, act_ext, f_all, far_act, right_l2, far_l2, right_l1, far_l1, out):
    nx, ny, nz, units = parts
    rows = act_b.shape[0]
    tiles = right_l2.shape[1] // 128
    count = 9 * tiles

    def emit(left_own, left_far, right_own, right_far, left_at, right_at, lead_x):
        for k in range(3):
            a, b = left_at(k), right_at(k)
            total = dot_tn(left_own[a : a + rows], right_own[b : b + rows])
            total = total + dot_tn(left_far[a : a + rows], right_far[b : b + rows])
            for j in range(tiles):
                tile = total[:, j * 128 : (j + 1) * 128].astype(BF16).reshape(nx, nz, 3, 8, 128)
                for g in range(3):
                    unit = (k * tiles + j) * 3 + g
                    y, i = unit // units, unit % units
                    if lead_x:
                        out[:, y, :, i] = tile[:, :, g]
                    else:
                        out[y, :, :, i] = tile[:, :, g]
        for unit in range(count, ny * units):
            y, i = unit // units, unit % units
            blank = jnp.zeros((nx, nz, 8, 128), BF16)
            if lead_x:
                out[:, y, :, i] = blank
            else:
                out[y, :, :, i] = blank

    @pl.when(core[0] == 0)
    def _():
        emit(act_b, f_all, right_l2, far_l2, lambda k: 0, lambda k: (2 - k) * SECOND, True)

    @pl.when(core[0] != 0)
    def _():
        emit(act_ext, far_act, right_l1, far_l1, lambda k: k * FIRST, lambda k: 0, False)


def weights(parts, start, width, core, act_b, act_ext, f_all, far_act, far_cot, grad_m, cot_ext):
    rows, ch = act_b.shape
    nx, ny, nz, units = parts
    cols = lambda a: pl.BlockSpec(
        (a.shape[0], width), lambda n: (0, start // width), pipeline_mode=pl.Buffered(1)
    )
    shape = (nx, ny, nz, units, 8, 128)
    return pl.pallas_call(
        lambda *refs: weight_kernel(parts, *refs),
        grid=(1,),
        in_specs=[
            pl.BlockSpec(memory_space=pltpu.SMEM),
            once(act_b),
            once(act_ext),
            once(f_all),
            once(far_act),
            cols(cot_ext),
            cols(far_cot),
            cols(grad_m),
            cols(f_all),
        ],
        out_specs=pl.BlockSpec(shape, lambda n: (0,) * 6),
        out_shape=pltpu.VMEM(shape, BF16),
        compiler_params=pltpu.CompilerParams(vmem_limit_bytes=20 << 20),
        cost_estimate=pl.CostEstimate(
            flops=12 * rows * ch * width, transcendentals=0, bytes_accessed=12 * ch * width
        ),
        name="weights",
    )(core, act_b, act_ext, f_all, far_act, cot_ext, far_cot, grad_m, f_all)


def exchange(data, order, core_axis, token=None):
    axes = ("x", "z", "y", "c")
    sizes = [lax.axis_size(a) for a in axes]
    n = data.shape[0]
    rest = data.shape[1:]

    def pairs(k):
        found = []
        for i in range(math.prod(sizes)):
            place = list(np.unravel_index(i, sizes))
            at = axes.index(core_axis[place[3]])
            place[at] = (place[at] + k) % n
            found.append((i, int(np.ravel_multi_index(place, sizes))))
        return found

    total = None
    for k in (0, *range(2, n - 1), 1, n - 1):
        chunk = lax.dynamic_slice(
            data, (order[k],) + (0,) * len(rest), (1,) + rest, allow_negative_indices=False
        ).reshape(rest)
        if k:
            chunk = lax.ppermute(chunk, axes, pairs(k))
        if k == 2 and token is not None:
            chunk, token = lax.optimization_barrier((chunk, token))
        chunk = chunk.astype(F32)
        total = chunk if total is None else total + chunk
    return total.astype(BF16), token


def order_of(me, n):
    return [jnp.where(me + k < n, me + k, me + k - n) for k in range(n)]


def neighbours(low, high):
    axes = ("x", "z")
    count = lax.axis_size("x") * lax.axis_size("z")
    forward = [(i, i + 1) for i in range(count - 1)]
    backward = [(t, s) for s, t in forward]
    return lax.ppermute(high, axes, forward), lax.ppermute(low, axes, backward)


def per_device(signal, w1, w2, cotangent):
    sig, cot = signal[0], cotangent[0]
    rows, ch = sig.shape
    nx, ny, nz = (lax.axis_size(a) for a in ("x", "y", "z"))
    tokens = signal.shape[0] * ny * lax.axis_size("c") * rows * nx * nz
    scale = 1.0 / math.sqrt(tokens)
    splits = [(0, ch)]
    sizes = [9 * width // 128 for _, width in splits]
    units = [-(-size // ny) for size in sizes]
    core = lax.axis_index("c").astype(jnp.int32).reshape(1)
    place = lax.axis_index("x") * nz + lax.axis_index("z")
    inside = jnp.stack([place > 0, place < nx * nz - 1]).astype(jnp.int32)

    at_x, at_y = (lax.axis_index(a).astype(jnp.int32) for a in ("x", "y"))
    order_a = order_of(jnp.where(core[0] == 0, at_x, at_y), nx)
    order_b = order_of(jnp.where(core[0] == 0, at_y, at_x), ny)
    sig, cot, core, inside, order_a, order_b = lax.optimization_barrier(
        (sig, cot, core, inside, order_a, order_b)
    )

    low, high, low_far, high_far = edges(sig, cot)
    lo, hi = neighbours(low, high)
    lo_far, hi_far = neighbours(low_far, high_far)
    act = lambda v: gelu(v.astype(F32)).astype(BF16)
    act_ext = jnp.concatenate([act(lo[:FIRST]), act(sig), act(hi[:FIRST])])
    cot_ext = jnp.concatenate([lo[FIRST:], cot, hi[FIRST:]])
    swap = lambda a: lax.ppermute(a, "c", [(0, 1), (1, 0)])
    far_act, far_cot = swap(act_ext), swap(cot_ext)
    cot_ext, lo_far, hi_far = lax.optimization_barrier((cot_ext, lo_far, hi_far))
    mid, act_b, grad_m, give = front(core, act_ext, cot_ext, sig, cot, w1, w2)
    f_all = swap(give)
    pieces = [
        weights((nx, ny, nz, u), *split, core, act_b, act_ext, f_all, far_act, far_cot, grad_m, cot_ext)
        for split, u in zip(splits, units)
    ]
    piece, inside = lax.optimization_barrier((pieces[0], inside))
    pieces = [exchange(piece, order_a, "xy")[0]]
    lo2, hi2 = wings(inside, act_ext, cot_ext, lo, hi, lo_far, hi_far, w1, w2)
    output, grad_s = back(act_b, lo2, hi2, grad_m, mid, sig, w1, w2)
    pieces, output, grad_s = lax.optimization_barrier((pieces, output, grad_s))
    part, _ = exchange(jnp.concatenate(pieces, axis=2), order_b, "yx")

    got = lax.all_to_all(part, "z", 0, 0, tiled=True)
    part = jnp.sum(got.astype(F32), axis=0).astype(BF16)
    both = lax.all_to_all(
        jnp.broadcast_to(part[None], (2 * ny,) + part.shape), ("y", "c"), 0, 0, tiled=True
    )
    both = both.reshape((ny, 2) + part.shape).astype(F32) * scale

    def assemble(layer):
        found, at = [], 0
        for (_, width), size, u in zip(splits, sizes, units):
            flat = both[:, layer, at : at + u].reshape(ny * u, 8, 128)[:size]
            flat = flat.reshape(3, width // 128, 3, 8, 128).transpose(0, 2, 3, 1, 4)
            found.append(flat.reshape(3, 24, width))
            at += u
        return jnp.concatenate(found, axis=2)

    return output[None], grad_s[None], assemble(1), assemble(0)


def solution(mesh):
    fine = Mesh(mesh.devices.reshape(4, 8, 4, 2), ("x", "z", "y", "c"))
    placed = P(("y", "c"), ("x", "z"), None)
    split = P(None, ("x", "z"), None)
    return jax.shard_map(
        per_device,
        mesh=fine,
        in_specs=(placed, P(), P(), placed),
        out_specs=(placed, placed, split, split),
        check_vma=False,
    )
```
